32 devices in a mesh: patch: 2 (over y), tile: 8 (over z, core), row: 2 (over x), band: 1.
Axes of the slice: x: 2, y: 2, z: 4, core: 2. Of those that a mesh axis runs over, the one named last changes fastest.
Arguments:
- stamps: bfloat16 [768, 64, 128], P(('patch', 'tile', 'row', 'band')), parts along dimension 0, may hold values from -6 to 6
- variance: bfloat16 [768, 64, 128], P(('patch', 'tile', 'row', 'band')), parts along dimension 0, may hold values from 0.25 to 4
- basis_v: bfloat16 [21, 41], replicated, may hold values from -1 to 1
- basis_u: bfloat16 [21, 41], replicated, may hold values from -1 to 1
- coefficients: float32 [800, 21], P('patch'), parts along dimension 0, may hold values from 0.03 to 0.3
- coef_index: int32 [768], P(('patch', 'tile', 'row', 'band')), parts along dimension 0, may hold values from 0 to 399
- tile_dest: int32 [768], P(('patch', 'tile', 'row', 'band')), parts along dimension 0, may hold values from 0 to 7, as said below
- row_offset: int32 [768], P(('patch', 'tile', 'row', 'band')), parts along dimension 0, may hold values from 0 to 448
- sub_pixel: int32 [768, 2], P(('patch', 'tile', 'row', 'band')), parts along dimension 0, may hold values from 0 to 63
Outputs:
- coadd: float32 [8192, 128], P(('patch', 'tile', 'row', 'band')), parts along dimension 0
The draws below stay inside these ranges and needn't reach their ends.
There are 2 independent parts, one for each index of `patch`. The reference program is written for one: setup_inputs(seed, part) draws one part's arguments, and reference() takes and returns one part's arrays. A program takes and returns all parts, laid end to end along the dimension named above; an argument that names none is the same for every part. Nothing has to cross between parts.
Inputs may be any that keep to these rules, and one draw needn't show every extreme that they name: `tile_dest`: among the 24 stamps of one device at most 3 name the same tile, and one tile is named by exactly 3 stamps of every device.
All inputs are finite; a program needn't handle non-finite values.
Results may differ from the reference program's by a relative error of at most 0.0055.
Values may be sent and summed in bfloat16 or wider, within the bound.
No kernel may reach another device: no remote copies, remote signals or barrier semaphores. Data moves between devices by JAX's collectives and lax.ppermute only.
A program may use at most 64 MiB of HBM per device.

```python
import math
import jax
import jax.numpy as jnp
from jax import lax

SH = 64
SW = 128
TAPS = 41
NB = 21
SUBSTEPS = 64
EXPOSURES = 400
STAMP_DEV = 24
TILE_ROWS = 512
CAP = 3
N_STAMP = 384
COADD_ROWS = 4096
N_TILE = 8


def draw_tile_dest(key, part):
    key_hot, key_rest = jax.random.split(key)
    hot_tile = jax.random.randint(key_hot, (), 0, N_TILE)
    others = (hot_tile + 1 + jnp.arange(N_TILE - 1)) % N_TILE
    others_pool = jnp.repeat(others, CAP)
    block_count = N_STAMP // STAMP_DEV

    def one_block(block_key):
        key_pick, key_order = jax.random.split(block_key)
        picks = jax.random.permutation(key_pick, others_pool)[:STAMP_DEV - CAP]
        listed = jnp.concatenate([jnp.zeros((CAP,), jnp.int32) + hot_tile, picks.astype(jnp.int32)])
        return jax.random.permutation(key_order, listed)
    blocks = jax.vmap(one_block)(jax.random.split(key_rest, block_count))
    return blocks.reshape(-1).astype(jnp.int32)


def set_ends(drawn, own_key, smallest, top_value):
    extent = drawn.shape
    place = [jax.random.randint(jax.random.fold_in(own_key, axis), (), 0, extent[axis]) for axis in range(len(extent))]
    drawn = drawn.at[tuple(place)].set(smallest)
    longest = extent.index(max(extent))
    place[longest] = (place[longest] + 1) % extent[longest]
    return drawn.at[tuple(place)].set(top_value)


def block_scale(own_key, shape, shards, smallest, high):
    def one(position, shards_of):
        steps = jax.random.uniform(jax.random.fold_in(jax.random.fold_in(own_key, 6), position), (shards_of,), jnp.float32, smallest / len(shards), high / len(shards))
        return jnp.repeat(jnp.exp(steps), shape[position] // shards_of).reshape((-1,) + (1,) * (len(shape) - position - 1))

    level = one(*shards[0])
    for cut in shards[1:]:
        level = level * one(*cut)
    return level


def centred(rng, dims, width, reach, cuts=(), kind=jnp.bfloat16):
    array = jax.random.normal(rng, dims, jnp.float32) * width
    if len(cuts) > 0:
        array = block_scale(rng, dims, cuts, -0.22, 0.18) * array
    return jnp.clip(array, min=-reach, max=reach).astype(kind)


def setup_inputs(seed: int = 0, part: int = 0) -> dict:
    arg_keys = jax.random.split(jax.random.key(seed), 10)
    own_keys = jax.random.split(jax.random.fold_in(arg_keys[9], part), 10)
    stamps = centred(own_keys[0], (N_STAMP, SH, SW), 1.0, 6.0, ((0, 16),))
    variance = jnp.clip(jnp.exp(math.log(4.0) - 2.7725887 * jax.random.uniform(own_keys[1], (N_STAMP, SH, SW), jnp.float32) ** block_scale(own_keys[1], (N_STAMP, SH, SW), ((0, 16),), -0.2, 0.2)), 0.25, 4.0).astype(jnp.bfloat16)
    basis_v = centred(arg_keys[2], (NB, TAPS), TAPS ** -0.5, 1.0)
    basis_u = centred(arg_keys[3], (NB, TAPS), TAPS ** -0.5, 1.0)
    coefficients = jnp.clip(jnp.exp(jax.random.uniform(own_keys[4], (EXPOSURES, NB), jnp.float32, math.log(0.03), math.log(0.3))), 0.03, 0.3)
    coef_index = set_ends(jax.random.randint(own_keys[5], (N_STAMP,), 0, EXPOSURES), jax.random.fold_in(own_keys[5], 1), 0, EXPOSURES - 1).astype(jnp.int32)
    tile_dest = draw_tile_dest(jax.random.fold_in(jax.random.fold_in(arg_keys[9], part), 71), part)
    row_offset = set_ends(jax.random.randint(own_keys[7], (N_STAMP,), 0, TILE_ROWS - SH + 1), jax.random.fold_in(own_keys[7], 1), 0, TILE_ROWS - SH).astype(jnp.int32)
    sub_pixel = set_ends(jax.random.randint(own_keys[8], (N_STAMP, 2), 0, SUBSTEPS), jax.random.fold_in(own_keys[8], 1), 0, SUBSTEPS - 1).astype(jnp.int32)
    return dict(stamps=stamps, variance=variance, basis_v=basis_v, basis_u=basis_u, coefficients=coefficients, coef_index=coef_index, tile_dest=tile_dest, row_offset=row_offset, sub_pixel=sub_pixel)


def band_tables(basis_v, basis_u, stamp_rows, stamp_cols):
    tap_count = basis_v.shape[1]
    half_width = (tap_count - 1) // 2
    row_ids = jnp.arange(stamp_rows).astype(jnp.int32)
    col_ids = jnp.arange(stamp_cols).astype(jnp.int32)
    tap_ids = jnp.arange(tap_count).astype(jnp.int32)
    lag_rows = row_ids[None, :] - row_ids[:, None] + half_width
    pick_rows = (lag_rows[None, :, :] == tap_ids[:, None, None]).astype(jnp.float32)
    vertical = jnp.einsum("ka,aij->kij", basis_v.astype(jnp.float32), pick_rows,
                          precision=lax.Precision.HIGHEST).astype(jnp.bfloat16)
    lag_cols = col_ids[:, None] - col_ids[None, :] + half_width
    pick_cols = (lag_cols[None, :, :] == tap_ids[:, None, None]).astype(jnp.float32)
    horizontal = jnp.einsum("ka,apq->pkq", basis_u.astype(jnp.float32), pick_cols,
                            precision=lax.Precision.HIGHEST).astype(jnp.bfloat16)
    return vertical, horizontal.reshape(stamp_cols, -1)


def bilinear(values, frac_rows, frac_cols):
    below = jnp.concatenate([values[:, 1:], values[:, -1:]], axis=1)
    mixed = (1.0 - frac_rows) * values + frac_rows * below
    beside = jnp.concatenate([mixed[:, :, 1:], mixed[:, :, -1:]], axis=2)
    return (1.0 - frac_cols) * mixed + frac_cols * beside


def reference(stamps, variance, basis_v, basis_u, coefficients, coef_index, tile_dest, row_offset, sub_pixel):
    stamp_total, stamp_rows, stamp_cols = stamps.shape
    nbasis = basis_v.shape[0]
    vertical, horiz_table = band_tables(basis_v, basis_u, stamp_rows, stamp_cols)
    group_size = math.gcd(stamp_total, 64)
    groups = stamp_total // group_size
    coef_all = coefficients[coef_index.astype(jnp.int32)]
    row_ids = jnp.arange(stamp_rows).astype(jnp.int32)

    def step(carry, operands):
        numer_all, denom_all = carry
        images, spreads, coef_part, dest, offset, shift = operands
        flattened = images.reshape(group_size * stamp_rows, stamp_cols)
        horizontal = jnp.dot(flattened, horiz_table, preferred_element_type=jnp.float32).astype(jnp.bfloat16)
        horizontal = horizontal.reshape(group_size, stamp_rows, nbasis, stamp_cols)
        vertical_out = jnp.einsum("kai,bikc->bkac", vertical.astype(jnp.float32), horizontal.astype(jnp.float32),
                                  precision=lax.Precision.HIGHEST)
        matched = jnp.sum(coef_part[:, :, None, None] * vertical_out, axis=1).astype(jnp.bfloat16)
        frac_rows = shift[:, 0].astype(jnp.float32)[:, None, None] / SUBSTEPS
        frac_cols = shift[:, 1].astype(jnp.float32)[:, None, None] / SUBSTEPS
        warped = bilinear(matched.astype(jnp.float32), frac_rows, frac_cols)
        spread = bilinear(spreads.astype(jnp.float32), frac_rows, frac_cols)
        weight = 1.0 / spread
        rows_at = (dest.astype(jnp.int32) * TILE_ROWS + offset.astype(jnp.int32))[:, None] + row_ids[None, :]
        rows_flat = rows_at.reshape(-1)
        numer_all = numer_all.at[rows_flat].add((weight * warped).reshape(-1, stamp_cols))
        denom_all = denom_all.at[rows_flat].add(weight.reshape(-1, stamp_cols))
        return (numer_all, denom_all), None

    start = (jnp.zeros((COADD_ROWS, stamp_cols), jnp.float32), jnp.zeros((COADD_ROWS, stamp_cols), jnp.float32))
    operands = (stamps.reshape(groups, group_size, stamp_rows, stamp_cols),
                variance.reshape(groups, group_size, stamp_rows, stamp_cols),
                coef_all.reshape(groups, group_size, nbasis),
                tile_dest.reshape(groups, group_size),
                row_offset.reshape(groups, group_size),
                sub_pixel.reshape(groups, group_size, 2))
    (numer_all, denom_all), _ = lax.scan(step, start, operands)
    return numer_all / (denom_all + 1.0)
```

```python
import functools

import jax
import jax.numpy as jnp
from jax import lax
from jax.experimental import pallas as pl
from jax.experimental.pallas import tpu as pltpu
from jax.sharding import PartitionSpec as P

SUBSTEPS = 64
TILE_ROWS = 512
META_ROWS = 16
SUB_BITS = SUBSTEPS.bit_length() - 1


SMEM = pl.BlockSpec(memory_space=pltpu.SMEM)
VMEM = pl.BlockSpec(memory_space=pltpu.VMEM)


def partner(index, step, count):
    if count & (count - 1) == 0:
        return index ^ step
    return (index + step) % count


def call(kernel, name, out_shape, in_specs, out_specs, scratch, flops, moved, *operands):
    return pl.pallas_call(
        kernel,
        name=name,
        out_shape=out_shape,
        in_specs=in_specs,
        out_specs=out_specs,
        scratch_shapes=scratch,
        cost_estimate=pl.CostEstimate(flops=flops, bytes_accessed=moved, transcendentals=0),
        compiler_params=pltpu.CompilerParams(vmem_limit_bytes=48 * 2**20),
    )(*operands)


def pack_kernel(geo, where, dest, offsets, sub_pixel, variance, *refs):
    blocks, order, counts = refs[: geo.outer], refs[geo.outer], refs[geo.outer + 1]
    for tile in range(geo.tiles):
        counts[tile] = 0
    for slot in range(geo.tiles * geo.capacity):
        order[slot] = -1
    for stamp in range(geo.stamps):
        tile = dest[stamp]
        rank = counts[tile]
        order[tile * geo.capacity + rank] = stamp
        counts[tile] = rank + 1
    row_ids = lax.broadcasted_iota(jnp.int32, (META_ROWS, geo.cols), 0)
    lane_ids = lax.broadcasted_iota(jnp.int32, (META_ROWS, geo.cols), 1)
    for step in range(geo.outer):
        first = partner(where[0], step, geo.outer) * geo.block_slots
        meta = jnp.zeros((META_ROWS, geo.cols), jnp.int32)
        for slot in range(geo.block_slots):
            stamp = order[first + slot]
            safe = jnp.maximum(stamp, 0)
            blocks[step][slot * geo.rows : (slot + 1) * geo.rows, :] = variance[safe]
            code = ((offsets[safe] + 1) << (2 * SUB_BITS)) | (sub_pixel[0, safe] << SUB_BITS)
            code = jnp.where(stamp >= 0, code | sub_pixel[1, safe], 0)
            for row, part in enumerate((code >> 14, (code >> 7) & 127, code & 127)):
                meta = jnp.where((row_ids == row) & (lane_ids == slot), part, meta)
        blocks[step][geo.block_slots * geo.rows :, :] = meta.astype(jnp.float32).astype(
            jnp.bfloat16
        )


def match_kernel(geo, where, order, coef_index, stamps, basis_v, basis_u, coefs, *refs):
    blocks = refs[: geo.outer]
    vert, horiz, mixed, scales = refs[geo.outer :]
    nbasis, taps = basis_v.shape
    half = (taps - 1) // 2
    rows, cols = geo.rows, geo.cols
    tap_ids = lax.broadcasted_iota(jnp.int32, (taps, cols), 0)
    lane_ids = lax.broadcasted_iota(jnp.int32, (taps, cols), 1)
    pick_v = (tap_ids == (lane_ids + half) % cols).astype(jnp.bfloat16)
    pick_u = (tap_ids == (half - lane_ids + cols) % cols).astype(jnp.bfloat16)
    base_v = jnp.dot(basis_v[...], pick_v, preferred_element_type=jnp.float32)
    base_u = jnp.dot(basis_u[...], pick_u, preferred_element_type=jnp.float32)
    lag = lax.broadcasted_iota(jnp.int32, (cols, cols), 0) - lax.broadcasted_iota(
        jnp.int32, (cols, cols), 1
    )
    near = jnp.abs(lag) <= half
    for k in range(nbasis):
        line = jnp.broadcast_to(base_v[k : k + 1, :], (rows, cols))
        rolled = pltpu.roll(line, 0, 1, stride=1, stride_axis=0)
        vert[k * rows : (k + 1) * rows, :] = rolled[:, :rows].astype(jnp.bfloat16)
        line = jnp.broadcast_to(base_u[k : k + 1, :], (cols, cols))
        rolled = pltpu.roll(line, 0, 1, stride=1, stride_axis=0)
        horiz[k * cols : (k + 1) * cols, :] = jnp.where(near, rolled, 0.0).astype(jnp.bfloat16)

    exposure_ids = lax.broadcasted_iota(jnp.int32, coefs.shape, 1)
    chunk = 7 if nbasis % 7 == 0 else 1

    def one_pair(pair, carry):
        halves = []
        for side in range(2):
            slot = pair * 2 + side
            step = slot // geo.block_slots
            tile_slot = partner(where[0], step, geo.outer) * geo.block_slots
            stamp = jnp.maximum(order[tile_slot + slot % geo.block_slots], 0)
            halves.append(stamps[stamp])
            picked = jnp.where(exposure_ids == coef_index[stamp], coefs[...], 0.0)
            scales[side] = jnp.broadcast_to(
                jnp.sum(picked, axis=1, keepdims=True), (nbasis, cols)
            )
        both = jnp.concatenate(halves, axis=1)
        for begin in range(0, nbasis, chunk):
            product = jnp.dot(
                vert[begin * rows : (begin + chunk) * rows, :],
                both,
                preferred_element_type=jnp.float32,
            )
            for k in range(begin, begin + chunk):
                for side in range(2):
                    part = product[
                        (k - begin) * rows : (k - begin + 1) * rows,
                        side * cols : (side + 1) * cols,
                    ]
                    scaled = part * scales[side, k : k + 1, :]
                    mixed[
                        pl.ds(pl.multiple_of((pair * 2 + side) * rows, rows), rows),
                        k * cols : (k + 1) * cols,
                    ] = scaled.astype(jnp.bfloat16)
        return carry

    lax.fori_loop(0, geo.outer * geo.block_slots // 2, one_pair, 0)
    height = geo.block_slots * rows
    for step in range(geo.outer):
        blocks[step][...] = jnp.dot(
            mixed[step * height : (step + 1) * height, :],
            horiz[...],
            preferred_element_type=jnp.float32,
        ).astype(jnp.bfloat16)


def bilinear(values, frac_rows, frac_cols):
    rows, cols = values.shape
    row_ids = lax.broadcasted_iota(jnp.int32, values.shape, 0)
    lane_ids = lax.broadcasted_iota(jnp.int32, values.shape, 1)
    below = jnp.where(row_ids == rows - 1, values, pltpu.roll(values, rows - 1, 0))
    mixed = (1.0 - frac_rows) * values + frac_rows * below
    beside = jnp.where(lane_ids == cols - 1, mixed, pltpu.roll(mixed, cols - 1, 1))
    return (1.0 - frac_cols) * mixed + frac_cols * beside


def fractions(code):
    mask = SUBSTEPS - 1
    frac_rows = ((code >> SUB_BITS) & mask).astype(jnp.float32) * (1.0 / SUBSTEPS)
    frac_cols = (code & mask).astype(jnp.float32) * (1.0 / SUBSTEPS)
    return frac_rows, frac_cols


def add_at(total, geo, slot, code, values):
    base = (slot // geo.capacity) * TILE_ROWS
    start = base + (code >> (2 * SUB_BITS)) - 1
    total[pl.ds(start, geo.rows), :] = total[pl.ds(start, geo.rows), :] + values


def hand_out(geo, place, total, own, sends):
    share = geo.share
    own[...] = total[pl.ds(pl.multiple_of(place * share, share), share), :]
    for step, send in enumerate(sends, 1):
        start = pl.multiple_of(partner(place, step, geo.peers) * share, share)
        send[...] = total[pl.ds(start, share), :].astype(jnp.bfloat16)


def weight_kernel(geo, where, *refs):
    blocks = refs[: geo.outer]
    codes, weights, own = refs[geo.outer : geo.outer + 3]
    sends, total = refs[geo.outer + 3 : -1], refs[-1]
    total[...] = jnp.zeros_like(total)
    lane_ids = lax.broadcasted_iota(jnp.int32, (1, geo.cols), 1)
    for step in range(geo.outer):
        meta = blocks[step][geo.block_slots * geo.rows :, :].astype(jnp.float32)
        line = meta[0:1] * 16384.0 + meta[1:2] * 128.0 + meta[2:3]
        for slot in range(geo.block_slots):
            code = jnp.sum(jnp.where(lane_ids == slot, line, 0.0)).astype(jnp.int32)
            codes[step * geo.block_slots + slot] = code

    for step in range(geo.outer):
        for slot in range(geo.block_slots):
            code = codes[step * geo.block_slots + slot]

            @pl.when(code > 0)
            def _(step=step, slot=slot, code=code):
                spread = blocks[step][slot * geo.rows : (slot + 1) * geo.rows, :]
                weight = 1.0 / bilinear(spread.astype(jnp.float32), *fractions(code))
                weights[step * geo.block_slots + slot] = weight
                add_at(total, geo, slot, code, weight)

    hand_out(geo, where[1], total, own, sends)


def numer_kernel(geo, where, codes, weights, *refs):
    blocks = refs[: geo.outer]
    own, sends, total = refs[geo.outer], refs[geo.outer + 1 : -1], refs[-1]
    total[...] = jnp.zeros_like(total)
    for step in range(geo.outer):
        for slot in range(geo.block_slots):
            code = codes[step * geo.block_slots + slot]

            @pl.when(code > 0)
            def _(step=step, slot=slot, code=code):
                image = blocks[step][slot * geo.rows : (slot + 1) * geo.rows, :]
                warped = bilinear(image.astype(jnp.float32), *fractions(code))
                add_at(total, geo, slot, code, weights[step * geo.block_slots + slot] * warped)

    hand_out(geo, where[1], total, own, sends)


def final_kernel(geo, *refs):
    count = geo.peers
    numer, denom, out = refs[0][...], refs[count][...], refs[-1]
    for step in range(1, count):
        numer = numer + refs[step][...].astype(jnp.float32)
        denom = denom + refs[count + step][...].astype(jnp.float32)
    out[...] = numer / (denom + 1.0)


class Geometry:
    def __init__(self, mesh, stamps):
        self.tiles = mesh.shape["tile"]
        self.spread = mesh.shape["row"] * mesh.shape["band"]
        self.inner = 2 if self.tiles % 2 == 0 else 1
        self.outer = self.tiles // self.inner
        self.peers = self.inner * self.spread
        self.share = TILE_ROWS // self.spread
        self.stamps, self.rows, self.cols = stamps
        self.capacity = max(2, (self.stamps + self.tiles - 1) // self.tiles)
        self.block_slots = self.inner * self.capacity


def local(
    mesh, stamps, variance, basis_v, basis_u, coefficients, coef_index, tile_dest, row_offset,
    sub_pixel,
):
    geo = Geometry(mesh, stamps.shape)
    nbasis = basis_v.shape[0]
    axes = ("tile", "row", "band")
    position = lax.axis_index(axes)
    where = jnp.stack([position // geo.peers, position % geo.peers]).astype(jnp.int32)
    height = geo.block_slots * geo.rows
    slots = geo.outer * geo.block_slots
    shape = jax.ShapeDtypeStruct

    def between_groups(block, step):
        pairs = [
            (a * geo.peers + p, partner(a, step, geo.outer) * geo.peers + p)
            for a in range(geo.outer)
            for p in range(geo.peers)
        ]
        return lax.ppermute(block, axes, pairs)

    def within_group(block, step):
        pairs = [
            (a * geo.peers + p, a * geo.peers + partner(p, step, geo.peers))
            for a in range(geo.outer)
            for p in range(geo.peers)
        ]
        return lax.ppermute(block, axes, pairs)

    def travel(blocks):
        return [blocks[0]] + [between_groups(b, m) for m, b in enumerate(blocks) if m > 0]

    packed = call(
        functools.partial(pack_kernel, geo),
        "pack",
        [shape((height + META_ROWS, geo.cols), jnp.bfloat16)] * geo.outer
        + [shape((geo.tiles * geo.capacity,), jnp.int32)],
        [SMEM, SMEM, SMEM, SMEM, VMEM],
        [VMEM] * geo.outer + [SMEM],
        [pltpu.SMEM((geo.tiles,), jnp.int32)],
        1000,
        2 * variance.size * 2,
        where,
        tile_dest,
        row_offset,
        sub_pixel.T,
        variance,
    )
    order = packed[-1]
    spreads = travel(packed[:-1])
    matched = call(
        functools.partial(match_kernel, geo),
        "match",
        [shape((height, geo.cols), jnp.bfloat16)] * geo.outer,
        [SMEM, SMEM, SMEM, VMEM, VMEM, VMEM, VMEM],
        [VMEM] * geo.outer,
        [
            pltpu.VMEM((nbasis * geo.rows, geo.rows), jnp.bfloat16),
            pltpu.VMEM((nbasis * geo.cols, geo.cols), jnp.bfloat16),
            pltpu.VMEM((slots * geo.rows, nbasis * geo.cols), jnp.bfloat16),
            pltpu.VMEM((2, nbasis, geo.cols), jnp.float32),
        ],
        2 * slots * geo.rows * nbasis * geo.cols * (geo.rows + geo.cols),
        2 * stamps.size * 2,
        where,
        order,
        coef_index,
        stamps,
        basis_v,
        basis_u,
        coefficients.T,
    )
    images = travel(matched)
    sums = [shape((geo.share, geo.cols), jnp.float32)] + [
        shape((geo.share, geo.cols), jnp.bfloat16)
    ] * (geo.peers - 1)
    total = [pltpu.VMEM((geo.inner * TILE_ROWS, geo.cols), jnp.float32)]
    codes, weights, *denoms = call(
        functools.partial(weight_kernel, geo),
        "weigh",
        [shape((slots,), jnp.int32), shape((slots, geo.rows, geo.cols), jnp.float32)] + sums,
        [SMEM] + [VMEM] * geo.outer,
        [SMEM, VMEM] + [VMEM] * geo.peers,
        total,
        20 * slots * geo.rows * geo.cols,
        slots * geo.rows * geo.cols * 6,
        where,
        *spreads,
    )
    denoms = list(denoms[:1]) + [within_group(d, m) for m, d in enumerate(denoms) if m > 0]
    numers = call(
        functools.partial(numer_kernel, geo),
        "numer",
        sums,
        [SMEM, SMEM, VMEM] + [VMEM] * geo.outer,
        [VMEM] * geo.peers,
        total,
        20 * slots * geo.rows * geo.cols,
        slots * geo.rows * geo.cols * 6,
        where,
        codes,
        weights,
        *images,
    )
    numers = list(numers[:1]) + [within_group(d, m) for m, d in enumerate(numers) if m > 0]
    return call(
        functools.partial(final_kernel, geo),
        "final",
        shape((geo.share, geo.cols), jnp.float32),
        [VMEM] * (2 * geo.peers),
        VMEM,
        [],
        10 * geo.share * geo.cols,
        16 * geo.share * geo.cols,
        *numers,
        *denoms,
    )


def solution(mesh):
    split = ("patch", "tile", "row", "band")
    in_specs = (
        P(split, None, None),
        P(split, None, None),
        P(),
        P(),
        P("patch", None),
        P(split),
        P(split),
        P(split),
        P(split, None),
    )
    return jax.shard_map(
        functools.partial(local, mesh),
        mesh=mesh,
        in_specs=in_specs,
        out_specs=P(split, None),
        check_vma=False,
    )
```

```python
import functools

import jax
import jax.numpy as jnp
from jax import lax
from jax.experimental import pallas as pl
from jax.experimental.pallas import tpu as pltpu
from jax.sharding import PartitionSpec as P


SUBSTEPS = 64
TILE_ROWS = 512
META_ROWS = 16
AXES = ("tile", "row", "band")
SUB_BITS = SUBSTEPS.bit_length() - 1


CHUNK = 7
MSPLIT = 2
SMEM = pl.BlockSpec(memory_space=pltpu.SMEM)
VMEM = pl.BlockSpec(memory_space=pltpu.VMEM)
HBM = pl.BlockSpec(memory_space=pltpu.HBM)


def partner(index, step, count):
    if count & (count - 1) == 0:
        return index ^ step
    return (index + step) % count


def call(kernel, out_shape, in_specs, out_specs, scratch, flops, moved, *operands):
    return pl.pallas_call(
        kernel,
        out_shape=out_shape,
        in_specs=in_specs,
        out_specs=out_specs,
        scratch_shapes=scratch,
        cost_estimate=pl.CostEstimate(flops=flops, bytes_accessed=moved, transcendentals=0),
        compiler_params=pltpu.CompilerParams(vmem_limit_bytes=48 * 2**20),
    )(*operands)


def pack_kernel(geo, names, *refs):
    sources, refs = dict(zip(names, refs)), refs[len(names) :]
    blocks, (order, exposures), refs = refs[: geo.outer], refs[geo.outer : geo.outer + 2], refs[geo.outer + 2 :]
    targets, (counts, arrived) = dict(zip(names, refs)), refs[len(names) :]
    copies = {
        name: pltpu.make_async_copy(sources[name], targets[name], arrived.at[i])
        for i, name in enumerate(names)
    }
    for copy in copies.values():
        copy.start()
    group = lax.axis_index("tile") // geo.inner
    dest, offsets, sub_pixel = targets["dest"], targets["offsets"], targets["sub_pixel"]
    for tile in range(geo.tiles):
        counts[tile] = 0
    slots = geo.tiles * geo.capacity
    if slots != geo.stamps:
        for slot in range(slots):
            order[slot] = -1
    copies["dest"].wait()
    for stamp in range(geo.stamps):
        tile = dest[stamp]
        rank = counts[tile]
        order[tile * geo.capacity + rank] = stamp
        counts[tile] = rank + 1
    copies["coef_index"].wait()
    for slot in range(slots):
        exposures[slot] = targets["coef_index"][jnp.maximum(order[slot], 0)]
    row_ids = lax.broadcasted_iota(jnp.int32, (META_ROWS, geo.cols), 0)
    lane_ids = lax.broadcasted_iota(jnp.int32, (META_ROWS, geo.cols), 1)
    copies["offsets"].wait()
    copies["sub_pixel"].wait()
    copies["variance"].wait()
    for step in range(geo.outer):
        first = partner(group, step, geo.outer) * geo.block_slots
        meta = jnp.zeros((META_ROWS, geo.cols), jnp.int32)
        for slot in range(geo.block_slots):
            stamp = order[first + slot]
            safe = jnp.maximum(stamp, 0)
            blocks[step][slot * geo.rows : (slot + 1) * geo.rows, :] = targets["variance"][safe]
            code = ((offsets[safe] + 1) << (2 * SUB_BITS)) | (sub_pixel[0, safe] << SUB_BITS)
            code = jnp.where(stamp >= 0, code | sub_pixel[1, safe], 0)
            for row, part in enumerate((code >> 14, (code >> 7) & 127, code & 127)):
                meta = jnp.where((row_ids == row) & (lane_ids == slot), part, meta)
        blocks[step][geo.block_slots * geo.rows :, :] = meta.astype(jnp.float32).astype(
            jnp.bfloat16
        )
    for name in names[5:]:
        copies[name].wait()


def make_tables(geo, basis_v, basis_u, vert, horiz):
    nbasis, taps = basis_v.shape
    half = (taps - 1) // 2
    rows, cols = geo.rows, geo.cols
    tap_ids = lax.broadcasted_iota(jnp.int32, (taps, cols), 0)
    lane_ids = lax.broadcasted_iota(jnp.int32, (taps, cols), 1)
    pick_v = (tap_ids == (lane_ids + half) % cols).astype(jnp.bfloat16)
    pick_u = (tap_ids == (half - lane_ids + cols) % cols).astype(jnp.bfloat16)
    base_v = jnp.dot(basis_v[...], pick_v, preferred_element_type=jnp.float32)
    base_u = jnp.dot(basis_u[...], pick_u, preferred_element_type=jnp.float32)
    lag = lax.broadcasted_iota(jnp.int32, (cols, cols), 0) - lax.broadcasted_iota(
        jnp.int32, (cols, cols), 1
    )
    near = jnp.abs(lag) <= half
    for k in range(nbasis):
        line = jnp.broadcast_to(base_v[k : k + 1, :], (rows, cols))
        rolled = pltpu.roll(line, 0, 1, stride=1, stride_axis=0)
        vert[k * rows : (k + 1) * rows, :] = rolled[:, :rows].astype(jnp.bfloat16)
        line = jnp.broadcast_to(base_u[k : k + 1, :], (cols, cols))
        rolled = pltpu.roll(line, 0, 1, stride=1, stride_axis=0)
        horiz[k * cols : (k + 1) * cols, :] = jnp.where(near, rolled, 0.0).astype(jnp.bfloat16)


def first_match_kernel(geo, steps, order, exposures, stamps, coefs, basis_v, basis_u, *refs):
    vert, horiz = refs[:2]
    make_tables(geo, basis_v, basis_u, vert, horiz)
    match_kernel(geo, steps, order, exposures, stamps, coefs, vert, horiz, *refs[2:])


def match_kernel(geo, steps, order, exposures, stamps, coefs, vert, horiz, *refs):
    blocks, (mixed, scales) = refs[: len(steps)], refs[len(steps) :]
    nbasis = coefs.shape[0]
    rows, cols = geo.rows, geo.cols
    group = lax.axis_index("tile") // geo.inner
    exposure_ids = lax.broadcasted_iota(jnp.int32, coefs.shape, 1)
    chunk = CHUNK if nbasis % CHUNK == 0 else 1

    def one_pair(pair, carry):
        halves = []
        for side in range(2):
            slot = pair * 2 + side
            step = steps[0] + slot // geo.block_slots
            spot = partner(group, step, geo.outer) * geo.block_slots + slot % geo.block_slots
            halves.append(stamps[jnp.maximum(order[spot], 0)])
            picked = jnp.where(exposure_ids == exposures[spot], coefs[...], 0.0)
            scales[side] = jnp.broadcast_to(
                jnp.sum(picked, axis=1, keepdims=True), (nbasis, cols)
            )
        both = jnp.concatenate(halves, axis=1)
        for begin in range(0, nbasis, chunk):
            product = jnp.dot(
                vert[begin * rows : (begin + chunk) * rows, :],
                both,
                preferred_element_type=jnp.float32,
            )
            for k in range(begin, begin + chunk):
                for side in range(2):
                    part = product[
                        (k - begin) * rows : (k - begin + 1) * rows,
                        side * cols : (side + 1) * cols,
                    ]
                    scaled = part * scales[side, k : k + 1, :]
                    mixed[k, pl.ds(pl.multiple_of((pair * 2 + side) * rows, rows), rows), :] = (
                        scaled.astype(jnp.bfloat16)
                    )
        return carry

    lax.fori_loop(0, len(steps) * geo.block_slots // 2, one_pair, 0)
    height = geo.block_slots * rows
    band = height * len(steps) // MSPLIT
    for begin in range(0, height * len(steps), band):
        whole = jnp.concatenate([mixed[k, begin : begin + band, :] for k in range(nbasis)], axis=1)
        product = jnp.dot(whole, horiz[...], preferred_element_type=jnp.float32).astype(
            jnp.bfloat16
        )
        for at in range(0, band, rows):
            spot = begin + at
            blocks[spot // height][spot % height : spot % height + rows, :] = product[
                at : at + rows
            ]


def bilinear(values, frac_rows, frac_cols):
    rows, cols = values.shape
    row_ids = lax.broadcasted_iota(jnp.int32, values.shape, 0)
    lane_ids = lax.broadcasted_iota(jnp.int32, values.shape, 1)
    below = jnp.where(row_ids == rows - 1, values, pltpu.roll(values, rows - 1, 0))
    mixed = (1.0 - frac_rows) * values + frac_rows * below
    beside = jnp.where(lane_ids == cols - 1, mixed, pltpu.roll(mixed, cols - 1, 1))
    return (1.0 - frac_cols) * mixed + frac_cols * beside


def fractions(code):
    mask = SUBSTEPS - 1
    frac_rows = ((code >> SUB_BITS) & mask).astype(jnp.float32) * (1.0 / SUBSTEPS)
    frac_cols = (code & mask).astype(jnp.float32) * (1.0 / SUBSTEPS)
    return frac_rows, frac_cols


def for_live(geo, code, work):
    if geo.tiles * geo.capacity == geo.stamps:
        work()
    else:
        pl.when(code > 0)(work)


def add_at(total, geo, slot, code, values):
    base = (slot // geo.capacity) * TILE_ROWS
    start = base + (code >> (2 * SUB_BITS)) - 1
    total[pl.ds(start, geo.rows), :] = total[pl.ds(start, geo.rows), :] + values


def weight_kernel(geo, *refs):
    blocks, image = refs[: geo.outer], refs[geo.outer]
    codes, weights, denom, numer = refs[geo.outer + 1 :]
    denom[...] = jnp.zeros_like(denom)
    numer[...] = jnp.zeros_like(numer)
    lane_ids = lax.broadcasted_iota(jnp.int32, (1, geo.cols), 1)
    for step in range(geo.outer):
        meta = blocks[step][geo.block_slots * geo.rows :, :].astype(jnp.float32)
        line = meta[0:1] * 16384.0 + meta[1:2] * 128.0 + meta[2:3]
        for slot in range(geo.block_slots):
            code = jnp.sum(jnp.where(lane_ids == slot, line, 0.0)).astype(jnp.int32)
            codes[step * geo.block_slots + slot] = code
    for step in range(geo.outer):
        for slot in range(geo.block_slots):
            code = codes[step * geo.block_slots + slot]

            def work(step=step, slot=slot, code=code):
                spread = blocks[step][slot * geo.rows : (slot + 1) * geo.rows, :]
                weight = 1.0 / bilinear(spread.astype(jnp.float32), *fractions(code))
                weights[step * geo.block_slots + slot] = weight
                add_at(denom, geo, slot, code, weight)

            for_live(geo, code, work)
    add_images(geo, (0,), codes, weights, (image,), numer)


def add_images(geo, steps, codes, weights, blocks, total):
    for step, block in zip(steps, blocks):
        for slot in range(geo.block_slots):
            code = codes[step * geo.block_slots + slot]

            def work(step=step, slot=slot, code=code, block=block):
                image = block[slot * geo.rows : (slot + 1) * geo.rows, :]
                warped = bilinear(image.astype(jnp.float32), *fractions(code))
                add_at(total, geo, slot, code, weights[step * geo.block_slots + slot] * warped)

            for_live(geo, code, work)


def hand_out(place, count, sources, own, sends):
    share = own.shape[0] // len(sources)
    for i, source in enumerate(sources):
        rows = slice(i * share, (i + 1) * share)
        own[rows, :] = source[pl.ds(pl.multiple_of(place * share, share), share), :]
        for step, send in enumerate(sends, 1):
            start = pl.multiple_of(partner(place, step, count) * share, share)
            send[rows, :] = source[pl.ds(start, share), :].astype(jnp.bfloat16)


def late_kernel(geo, steps, codes, weights, denom, before, *refs):
    blocks = refs[: len(steps)]
    own, sends, total = refs[len(steps)], refs[len(steps) + 1 : -1], refs[-1]
    total[...] = before[...]
    add_images(geo, steps, codes, weights, blocks, total)
    hand_out(lax.axis_index("tile") % geo.inner, geo.inner, (total, denom), own, sends)


def join_kernel(geo, mine, *refs):
    parts, (own, *sends), total = refs[: geo.inner - 1], refs[geo.inner - 1 : -1], refs[-1]
    value = mine[...]
    for part in parts:
        value = value + part[...].astype(jnp.float32)
    total[...] = value
    halves = (total.at[:TILE_ROWS], total.at[TILE_ROWS:])
    hand_out(lax.axis_index(AXES[1:]), geo.spread, halves, own, sends)


def final_kernel(geo, mine, *refs):
    parts, out = refs[:-1], refs[-1]
    total = mine[...]
    for part in parts:
        total = total + part[...].astype(jnp.float32)
    out[...] = total[: geo.share] / (total[geo.share :] + 1.0)


class Geometry:
    def __init__(self, mesh, stamps):
        self.tiles = mesh.shape["tile"]
        self.spread = mesh.shape["row"] * mesh.shape["band"]
        self.inner = 2 if self.tiles % 2 == 0 else 1
        self.outer = self.tiles // self.inner
        self.peers = self.inner * self.spread
        self.share = TILE_ROWS // self.spread
        self.stamps, self.rows, self.cols = stamps
        self.capacity = max(2, (self.stamps + self.tiles - 1) // self.tiles)
        self.block_slots = self.inner * self.capacity


def local(
    mesh, stamps, variance, basis_v, basis_u, coefficients, coef_index, tile_dest, row_offset,
    sub_pixel,
):
    geo = Geometry(mesh, stamps.shape)
    nbasis = basis_v.shape[0]
    height = geo.block_slots * geo.rows
    slots = geo.outer * geo.block_slots
    shape = jax.ShapeDtypeStruct

    def between_groups(block, step):
        pairs = [
            (a * geo.peers + p, partner(a, step, geo.outer) * geo.peers + p)
            for a in range(geo.outer)
            for p in range(geo.peers)
        ]
        return lax.ppermute(block, AXES, pairs)

    def within_group(blocks, width, count):
        received = [blocks[0]]
        for step in range(1, count):
            pairs = [
                (i, i - p * width + partner(p, step, count) * width)
                for i in range(geo.outer * geo.peers)
                for p in (i // width % count,)
            ]
            received.append(lax.ppermute(blocks[step], AXES, pairs))
        return received

    arguments = {
        "dest": (tile_dest, pltpu.SMEM),
        "coef_index": (coef_index, pltpu.SMEM),
        "offsets": (row_offset, pltpu.SMEM),
        "sub_pixel": (sub_pixel.T, pltpu.SMEM),
        "variance": (variance, pltpu.VMEM),
        "stamps": (stamps, pltpu.VMEM),
        "basis_v": (basis_v, pltpu.VMEM),
        "basis_u": (basis_u, pltpu.VMEM),
        "coefs": (coefficients.T, pltpu.VMEM),
    }
    names = tuple(arguments)
    packed = call(
        functools.partial(pack_kernel, geo, names),
        [shape((height + META_ROWS, geo.cols), jnp.bfloat16)] * geo.outer
        + [shape((geo.tiles * geo.capacity,), jnp.int32)] * 2
        + [shape(a.shape, a.dtype) for a, _ in arguments.values()],
        [HBM] * len(names),
        [VMEM] * geo.outer
        + [SMEM] * 2
        + [pl.BlockSpec(memory_space=space) for _, space in arguments.values()],
        [
            pltpu.SMEM((geo.tiles,), jnp.int32),
            pltpu.SemaphoreType.DMA((len(names),)),
        ],
        1000,
        2 * variance.size * 2,
        *(pltpu.with_memory_space_constraint(a, pltpu.HBM) for a, _ in arguments.values()),
    )
    order, exposures = packed[geo.outer : geo.outer + 2]
    stamps_here, basis_v_here, basis_u_here, coefs_here = packed[-4:]
    spreads = [packed[0]]
    for step in range(1, geo.outer):
        spreads.append(between_groups(packed[step], step))

    def match(kernel, steps, extra_shapes, *operands):
        part = len(steps) * geo.block_slots * geo.rows
        return list(
            call(
                functools.partial(kernel, geo, steps),
                extra_shapes + [shape((height, geo.cols), jnp.bfloat16)] * len(steps),
                [SMEM, SMEM, VMEM, VMEM, VMEM, VMEM],
                [VMEM] * (len(extra_shapes) + len(steps)),
                [
                    pltpu.VMEM((nbasis, part, geo.cols), jnp.bfloat16),
                    pltpu.VMEM((2, nbasis, geo.cols), jnp.float32),
                ],
                2 * part * nbasis * geo.cols * (geo.rows + geo.cols),
                stamps.size * 2,
                order,
                exposures,
                stamps_here,
                coefs_here,
                *operands,
            )
        )

    middle = (geo.outer + 1) // 2
    images = {}
    vert, horiz, *far = match(
        first_match_kernel,
        tuple(range(middle, geo.outer)),
        [
            shape((nbasis * geo.rows, geo.rows), jnp.bfloat16),
            shape((nbasis * geo.cols, geo.cols), jnp.bfloat16),
        ],
        basis_v_here,
        basis_u_here,
    )
    for step in range(middle, geo.outer):
        images[step] = between_groups(far[step - middle], step)
    near = match(match_kernel, tuple(range(middle)), [], vert, horiz)
    for step in range(1, middle):
        images[step] = between_groups(near[step], step)
    full = (geo.inner * TILE_ROWS, geo.cols)
    codes, weights, denom, before = call(
        functools.partial(weight_kernel, geo),
        [
            shape((slots,), jnp.int32),
            shape((slots, geo.rows, geo.cols), jnp.float32),
            shape(full, jnp.float32),
            shape(full, jnp.float32),
        ],
        [VMEM] * (geo.outer + 1),
        [SMEM, VMEM, VMEM, VMEM],
        [],
        20 * slots * geo.rows * geo.cols,
        slots * geo.rows * geo.cols * 6,
        *spreads,
        near[0],
    )
    late = tuple(range(1, geo.outer))
    sums = call(
        functools.partial(late_kernel, geo, late),
        [shape((2 * TILE_ROWS, geo.cols), jnp.float32)]
        + [shape((2 * TILE_ROWS, geo.cols), jnp.bfloat16)] * (geo.inner - 1),
        [SMEM, VMEM, VMEM, VMEM] + [VMEM] * len(late),
        [VMEM] * geo.inner,
        [pltpu.VMEM(full, jnp.float32)],
        20 * len(late) * height * geo.cols,
        len(late) * height * geo.cols * 6,
        codes,
        weights,
        denom,
        before,
        *(images[step] for step in late),
    )
    sums = within_group(sums, geo.spread, geo.inner)
    sums = call(
        functools.partial(join_kernel, geo),
        [shape((2 * geo.share, geo.cols), jnp.float32)]
        + [shape((2 * geo.share, geo.cols), jnp.bfloat16)] * (geo.spread - 1),
        [VMEM] * geo.inner,
        [VMEM] * geo.spread,
        [pltpu.VMEM((2 * TILE_ROWS, geo.cols), jnp.float32)],
        4 * TILE_ROWS * geo.cols,
        16 * TILE_ROWS * geo.cols,
        *sums,
    )
    sums = within_group(sums, 1, geo.spread)
    return call(
        functools.partial(final_kernel, geo),
        shape((geo.share, geo.cols), jnp.float32),
        [VMEM] * geo.spread,
        VMEM,
        [],
        10 * geo.share * geo.cols,
        16 * geo.share * geo.cols,
        *sums,
    )


def solution(mesh):
    split = ("patch", "tile", "row", "band")
    in_specs = (
        P(split, None, None),
        P(split, None, None),
        P(),
        P(),
        P("patch", None),
        P(split),
        P(split),
        P(split),
        P(split, None),
    )

    def body(*operands):
        return local(mesh, *operands)

    return jax.shard_map(
        body,
        mesh=mesh,
        in_specs=in_specs,
        out_specs=P(split, None),
        check_vma=False,
    )
```
